128 devices in a mesh: gx: 8 (over z, core), gy: 16 (over x, y).
Axes of the slice: x: 4, y: 4, z: 4, core: 2. Of those that a mesh axis runs over, the one named last changes fastest.
Arguments:
- state_prev: float32 [256, 128, 1024], P('gy', None, 'gx'), may hold values from -60 to 60
- diffusivity: float32 [256, 128, 1024], P('gy', None, 'gx'), may hold values from 0.5 to 4
- vapour: float32 [256, 128, 1024], P('gy', None, 'gx'), may hold values from 0.01 to 0.1
- cos_zenith: float32 [256, 1024], P('gy', 'gx'), may hold values from 0.1 to 1
- albedo: float32 [256, 1024], P('gy', 'gx'), may hold values from 0.05 to 0.8
- absorption: float32 [128, 112], replicated, may hold values from 0.005 to 1
- solar_weight: float32 [112], replicated, may hold values from 0.002 to 0.02
- day_mask: int32 [2048], P(('gx', 'gy')), may hold values from 0 to 1, as said below
Outputs:
- state_next: float32 [256, 128, 1024], P('gy', None, 'gx')
- residual: float32 [256, 128, 1024], P('gy', None, 'gx')
- net_flux: float32 [256, 128, 1024], P('gy', None, 'gx')
The draws below stay inside these ranges and needn't reach their ends.
Inputs may be any that keep to these rules, and one draw needn't show every extreme that they name: `day_mask`: exactly half of the 2048 entries are 1, and some device holds only sunlit blocks.
All inputs are finite; a program needn't handle non-finite values.
Results may differ from the reference program's by a relative error of at most 0.00015.
Values sent between devices are 32-bit elements; how exact they have to be, the bound alone decides.
No kernel may reach another device: no remote copies, remote signals or barrier semaphores. Data moves between devices by JAX's collectives and lax.ppermute only.
A program may use at most 128 MiB of HBM per device.

```python
import math
import jax
import jax.numpy as jnp
from jax import lax

CX = 128
LEV = 128
G = 112
ITERS = 5
NX = 1024
NY = 256
NBLK = 2048


def draw_state_prev(key, part):
    latitude = jnp.arange(NY, dtype=jnp.float32)[:, None, None]
    growth = 10.0 ** (latitude / max(NY - 1, 1))
    values = jax.random.normal(key, (NY, LEV, NX), jnp.float32) * growth
    return jnp.clip(values, -60.0, 60.0)


def draw_day_mask(key, part):
    tilt_key, noon_key = jax.random.split(jax.random.fold_in(key, 7))
    blocks_along = NBLK // NY
    tilt = jax.random.randint(tilt_key, (), 0, 2 * blocks_along + 1)
    noon = jax.random.randint(noon_key, (), 0, blocks_along)
    latitude = jnp.arange(NY, dtype=jnp.int32)
    slope = tilt * (2 * latitude + 1 - NY)
    half_width = blocks_along // 2
    offset_rows = jnp.sign(slope) * (jnp.abs(slope) // NY)
    day_width = half_width + jnp.clip(offset_rows, -half_width, half_width)
    longitude = jnp.arange(blocks_along, dtype=jnp.int32)
    distance = (longitude[:, None] - noon) % blocks_along
    sunlit = (distance < day_width[None, :]).astype(jnp.int32)
    return sunlit.reshape(NBLK)


def levels(own_key, extent, cuts, least, largest):
    gain, own = 1.0, jax.random.fold_in(own_key, 6)
    for position, parts in cuts:
        heights = jnp.exp(jax.random.uniform(jax.random.fold_in(own, position), (parts,), jnp.float32, least / len(cuts), largest / len(cuts)))
        gain = gain * jnp.repeat(heights, extent[position] // parts).reshape([-1 if axis == position else 1 for axis in range(len(extent))])
    return gain


def setup_inputs(seed: int = 0) -> dict:
    key_of = jax.random.split(jax.random.key(seed), 9)
    state_prev = draw_state_prev(jax.random.fold_in(key_of[8], 71), 0)
    diffusivity = jnp.clip(jnp.exp(math.log(4.0) - 2.0794415 * jax.random.uniform(key_of[1], (NY, LEV, NX), jnp.float32) ** levels(key_of[1], (NY, LEV, NX), ((0, 16), (2, 8)), -0.2, 0.2)), 0.5, 4.0)
    vapour = jnp.clip(jnp.exp(math.log(0.1) - 2.3025851 * jax.random.uniform(key_of[2], (NY, LEV, NX), jnp.float32) ** levels(key_of[2], (NY, LEV, NX), ((0, 16), (2, 8)), -0.2, 0.2)), 0.01, 0.1)
    cos_zenith = jnp.clip(0.1 + 0.9 * jax.random.uniform(key_of[3], (NY, NX), jnp.float32) ** levels(key_of[3], (NY, NX), ((0, 16), (1, 8)), -0.2, 0.2), 0.1, 1.0)
    albedo = jnp.clip(0.05 + 0.75 * jax.random.uniform(key_of[4], (NY, NX), jnp.float32) ** levels(key_of[4], (NY, NX), ((0, 16), (1, 8)), -0.2, 0.2), 0.05, 0.8)
    absorption = jnp.clip(jnp.exp(jax.random.uniform(key_of[5], (LEV, G), jnp.float32, math.log(0.005), math.log(1.0))), 0.005, 1.0)
    solar_weight = jnp.clip(jnp.exp(jax.random.uniform(key_of[6], (G,), jnp.float32, math.log(0.002), math.log(0.02))), 0.002, 0.02)
    day_mask = draw_day_mask(jax.random.fold_in(key_of[8], 71), 0)
    return dict(state_prev=state_prev, diffusivity=diffusivity, vapour=vapour, cos_zenith=cos_zenith, albedo=albedo, absorption=absorption, solar_weight=solar_weight, day_mask=day_mask)


def neighbours(values):
    widened = jnp.concatenate([values[:, :, -1:], values, values[:, :, :1]], 2)
    extended = jnp.pad(values, ((1, 1), (0, 0), (0, 0)))
    return (widened, extended)

def face_terms(diffusivity):
    widened, extended = neighbours(diffusivity)
    east_face = jnp.sqrt(diffusivity * widened[:, :, 2:])
    west_face = jnp.sqrt(diffusivity * widened[:, :, :-2])
    north_face = jnp.sqrt(diffusivity * extended[2:])
    south_face = jnp.sqrt(diffusivity * extended[:-2])
    level_face = jnp.sqrt(diffusivity[:, 1:] * diffusivity[:, :-1])
    return (east_face, west_face, north_face, south_face, level_face)

def operate(values, conductances):
    east_face, west_face, north_face, south_face, level_face = conductances
    widened, extended = neighbours(values)
    applied = values + east_face * (values - widened[:, :, 2:]) + west_face * (values - widened[:, :, :-2])
    applied = applied + north_face * (values - extended[2:]) + south_face * (values - extended[:-2])
    vertical = level_face * (values[:, 1:] - values[:, :-1])
    padding = jnp.zeros_like(values[:, :1])
    return applied - jnp.concatenate([vertical, padding], 1) + jnp.concatenate([padding, vertical], 1)

def reference(state_prev, diffusivity, vapour, cos_zenith, albedo, absorption, solar_weight, day_mask):
    conductances = face_terms(diffusivity)
    state_next = state_prev
    residual = state_prev - operate(state_prev, conductances)
    direction = residual
    current = jnp.sum(residual * residual)
    for iteration in range(ITERS):
        applied = operate(direction, conductances)
        step_size = current / jnp.sum(direction * applied)
        state_next = state_next + step_size * direction
        residual = residual - step_size * applied
        following = jnp.sum(residual * residual)
        direction = residual + following / current * direction
        current = following
    optical = vapour * (1.0 + 0.5 * jnp.tanh(state_prev))
    absorb32 = absorption.astype(jnp.float32)
    weight32 = solar_weight.astype(jnp.float32)

    def one_row(inputs):
        layer_amount, cosine, surface = inputs
        thickness = absorb32[:, :, None] * layer_amount[:, None, :]
        cumulative = jnp.cumsum(thickness, 0)
        downward = cosine * jnp.exp(-cumulative / cosine)
        upward = surface * downward[-1] * jnp.exp(-1.66 * (cumulative[-1] - cumulative))
        return jnp.einsum('lgc,g->lc', downward - upward, weight32, precision=lax.Precision.HIGHEST)
    fluxes = lax.map(one_row, (optical, cos_zenith, albedo))
    blocks_along = NBLK // NY
    lit_rows = jnp.repeat(day_mask.reshape(blocks_along, NY).T, CX, axis=1).astype(jnp.float32)
    net_flux = fluxes * lit_rows[:, None, :]
    return (state_next, residual, net_flux)
```

```python
import functools
import math

import jax
import jax.numpy as jnp
from jax import lax
from jax.experimental import pallas as pl
from jax.experimental.pallas import tpu as pltpu
from jax.sharding import PartitionSpec as P

ITERS = 5
DEPTH = ITERS + 1
SLOT = 8
PAD = 8
CHUNK = 32
CENTRE = 14.0
HALF = 13.0
TRUST = 500.0
LOG2E = math.log2(math.e)
GX, GY = ("gx", "gy")
F32 = jnp.float32


def ring(axis, step):
    n = lax.axis_size(axis)
    return [(i, (i + step) % n) for i in range(n)]


def line(axis, step):
    n = lax.axis_size(axis)
    return [(i, i + step) for i in range(n) if 0 <= i + step < n]


def lanes(shape):
    return lax.broadcasted_iota(jnp.int32, shape, len(shape) - 1)


def edges_kernel(state, diff, north, south, east, west):
    rows, levels, width = state.shape
    for f, source in enumerate((state, diff)):
        south[f * DEPTH : (f + 1) * DEPTH] = source[:DEPTH]
        north[f * DEPTH : (f + 1) * DEPTH] = source[rows - DEPTH :]

        @pl.loop(0, levels // CHUNK)
        def _(c):
            at = pl.ds(pl.multiple_of(c * CHUNK, CHUNK), CHUNK)
            lane = lanes((CHUNK, width))
            to_west = jnp.zeros((CHUNK, width), F32)
            to_east = jnp.zeros((CHUNK, width), F32)
            for r in range(rows):
                x = source[r, at, :]
                mine = (lane >= r * SLOT) & (lane < (r + 1) * SLOT)
                w = pltpu.roll(x, r * SLOT, 1) if r else x
                to_west = jnp.where(mine, w, to_west)
                e = pltpu.roll(x, (r * SLOT + DEPTH) % width, 1)
                to_east = jnp.where(mine, e, to_east)
            west[f, at, :] = to_west
            east[f, at, :] = to_east


def edges(state, diff):
    rows, levels, width = state.shape
    tall = jax.ShapeDtypeStruct((2 * DEPTH, levels, width), F32)
    thin = jax.ShapeDtypeStruct((2, levels, width), F32)
    return pl.pallas_call(
        edges_kernel,
        out_shape=(tall, tall, thin, thin),
        compiler_params=pltpu.CompilerParams(vmem_limit_bytes=24 << 20),
        cost_estimate=pl.CostEstimate(
            flops=1 << 20, bytes_accessed=4 << 20, transcendentals=0
        ),
        name="edges",
    )(state, diff)


def basis_kernel(
    state, diff, north, south, east, west, north_side, south_side, vectors, moments, *work
):
    ce, cn, cl, cu, va, vb, vc = work
    rows, levels, width = state.shape
    total = rows + 2 * DEPTH
    ring_buffers = (va, vb, vc)
    for buffer in ring_buffers:

        @pl.loop(0, total)
        def _(r):
            for t in range(2):
                buffer[r, t, :PAD, :] = jnp.zeros((PAD, width), F32)
                buffer[r, t, PAD + levels :, :] = jnp.zeros((PAD, width), F32)

    @pl.loop(0, levels // CHUNK)
    def _(c):
        at = pl.ds(pl.multiple_of(c * CHUNK, CHUNK), CHUNK)
        to = pl.ds(pl.multiple_of(c * CHUNK + PAD, PAD), CHUNK)
        lane = lanes((CHUNK, width))
        for f, (own, target) in enumerate(((state, va), (diff, vb))):
            for r in range(total):
                if r < DEPTH:
                    x = south[f * DEPTH + r, at, :]
                    e, w = south_side[f, at, :], south_side[2 + f, at, :]
                    slot = rows - DEPTH + r
                elif r < DEPTH + rows:
                    x = own[r - DEPTH, at, :]
                    e, w = east[f, at, :], west[f, at, :]
                    slot = r - DEPTH
                else:
                    slot = r - DEPTH - rows
                    x = north[f * DEPTH + slot, at, :]
                    e, w = north_side[f, at, :], north_side[2 + f, at, :]
                up = (width - slot * SLOT) % width
                e = pltpu.roll(e, up, 1) if up else e
                down = (2 * width - DEPTH - slot * SLOT) % width
                w = pltpu.roll(w, down, 1) if down else w
                side = jnp.where(lane < DEPTH, e, jnp.where(lane >= width - DEPTH, w, 0.0))
                if f:
                    x, side = jnp.sqrt(x), jnp.sqrt(side)
                target[r, 0, to, :] = x
                target[r, 1, to, :] = side

    def eastward(v0, v1):
        last = lanes(v0.shape) == width - 1
        a, b = pltpu.roll(v0, width - 1, 1), pltpu.roll(v1, width - 1, 1)
        return jnp.where(last, b, a), jnp.where(last, a, b)

    def westward(v0, v1):
        first = lanes(v0.shape) == 0
        a, b = pltpu.roll(v0, 1, 1), pltpu.roll(v1, 1, 1)
        return jnp.where(first, b, a), jnp.where(first, a, b)

    @pl.loop(0, total)
    def _(r):
        beyond = jnp.minimum(r + 1, total - 1)
        for c in range(levels // CHUNK):
            lo = PAD + c * CHUNK
            q = [vb[r, t, lo : lo + CHUNK, :] for t in range(2)]
            nearby = eastward(*q)
            for t in range(2):
                at = slice(c * CHUNK, (c + 1) * CHUNK)
                ce[r, t, at, :] = q[t] * nearby[t]
                cn[r, t, at, :] = q[t] * vb[beyond, t, lo : lo + CHUNK, :]
                cl[r, t, at, :] = q[t] * vb[r, t, lo + 1 : lo + CHUNK + 1, :]
                cu[r, t, at, :] = q[t] * vb[r, t, lo - 1 : lo + CHUNK - 1, :]

    def apply(k, source, older, target):
        def row(r, sums):
            own = sums is not None
            for c in range(levels // CHUNK):
                lo = PAD + c * CHUNK
                at = slice(c * CHUNK, (c + 1) * CHUNK)
                v = [source[r, t, lo : lo + CHUNK, :] for t in range(2)]
                nearby = eastward(*v)
                east_flux = [ce[r, t, at, :] * (v[t] - nearby[t]) for t in range(2)]
                west_flux = westward(*east_flux)
                for t in range(2):
                    spread = east_flux[t] - west_flux[t]
                    spread += cn[r, t, at, :] * (v[t] - source[r + 1, t, lo : lo + CHUNK, :])
                    spread += cn[r - 1, t, at, :] * (v[t] - source[r - 1, t, lo : lo + CHUNK, :])
                    spread += cl[r, t, at, :] * (v[t] - source[r, t, lo + 1 : lo + CHUNK + 1, :])
                    spread += cu[r, t, at, :] * (v[t] - source[r, t, lo - 1 : lo + CHUNK - 1, :])
                    if k == 0:
                        new = -spread
                    elif k == 1:
                        new = (spread + (1.0 - CENTRE) * v[t]) * (1.0 / HALF)
                    else:
                        new = (spread + (1.0 - CENTRE) * v[t]) * (2.0 / HALF)
                        new = new - older[r, t, lo : lo + CHUNK, :]
                    if k < ITERS:
                        target[r, t, lo : lo + CHUNK, :] = new
                    if own and t == 0:
                        vectors[k, r - DEPTH, at, :] = new
                        both = [new * new] if k < ITERS else []
                        if k:
                            both.append(new * v[0])
                        folded = [p.reshape(CHUNK // 8, 8, width).sum(0) for p in both]
                        sums = tuple(s + p for s, p in zip(sums, folded))
            return sums

        def halo(r):
            row(r, None)

        if k + 1 < DEPTH:
            pl.loop(k + 1, DEPTH)(halo)
            pl.loop(DEPTH + rows, total - 1 - k)(halo)
        count = 1 if k in (0, ITERS) else 2
        zero = jnp.zeros((8, width), F32)
        sums = lax.fori_loop(DEPTH, DEPTH + rows, row, (zero,) * count)
        first = [2 * k, 2 * k - 1] if k < ITERS else [2 * k - 1]
        for place, part in zip(first, sums):
            moments[place : place + 1, :] = jnp.sum(part, 0, keepdims=True)

    moments[...] = jnp.zeros_like(moments)
    apply(0, va, None, vb)
    order = (vb, vc, va)
    for k in range(1, DEPTH):
        apply(k, order[(k - 1) % 3], order[(k - 2) % 3], order[k % 3])


def basis(*arrays):
    rows, levels, width = arrays[0].shape
    total = rows + 2 * DEPTH
    return pl.pallas_call(
        basis_kernel,
        out_shape=(
            jax.ShapeDtypeStruct((DEPTH, rows, levels, width), F32),
            jax.ShapeDtypeStruct((16, width), F32),
        ),
        scratch_shapes=[pltpu.VMEM((total, 2, levels, width), F32)] * 4
        + [pltpu.VMEM((total, 2, levels + 2 * PAD, width), F32)] * 3,
        compiler_params=pltpu.CompilerParams(vmem_limit_bytes=48 << 20),
        cost_estimate=pl.CostEstimate(
            flops=100 << 20, bytes_accessed=14 << 20, transcendentals=0
        ),
        name="basis",
    )(*arrays)


def coefficients(sums):
    zero = jnp.zeros_like(sums[0])
    one = zero + 1.0
    mom = []
    for k in range(ITERS):
        mom.append(2.0 * sums[2 * k] - (mom[0] if k else sums[0]))
        mom.append(2.0 * sums[2 * k + 1] - (mom[1] if k else sums[1]))

    gram = {}
    for j in range(DEPTH):
        for k in range(j, DEPTH):
            if j + k < 2 * ITERS:
                gram[j, k] = gram[k, j] = 0.5 * (mom[j + k] + mom[k - j])

    def inner(a, b):
        value = size = zero
        for j, p in enumerate(a):
            for k, q in enumerate(b):
                term = p * q * gram[j, k]
                value, size = value + term, size + jnp.abs(term)
        return value, size

    def image(p):
        out = [CENTRE * q for q in p] + [zero]
        for k, q in enumerate(p):
            if k == 0:
                out[1] = out[1] + HALF * q
            else:
                out[k - 1] = out[k - 1] + 0.5 * HALF * q
                out[k + 1] = out[k + 1] + 0.5 * HALF * q
        return out

    def combined(a, scale, b):
        n = max(len(a), len(b))
        a, b = [list(x) + [zero] * (n - len(x)) for x in (a, b)]
        return [p + scale * q for p, q in zip(a, b)]

    residual, direction, field = [one], [one], []
    current, loss = mom[0], one
    for k in range(ITERS):
        applied = image(direction)
        curvature, size = inner(direction, applied)
        loss = jnp.maximum(loss, jnp.where(size < TRUST * curvature, one, 2.0 * one))
        step = current / curvature
        field = combined(field, step, direction)
        residual = combined(residual, -step, applied)
        if k < ITERS - 1:
            following, size = inner(residual, residual)
            loss = jnp.maximum(loss, jnp.where(size < TRUST * following, one, 2.0 * one))
            direction = combined(residual, following / current, direction)
            current = following
    return field, residual, loss


def recombine_kernel(moments, state, vectors, new_state, residual, loss, weights):
    @pl.when(pl.program_id(0) == 0)
    def _():
        width = moments.shape[1]
        sums = [
            jnp.broadcast_to(jnp.sum(moments[i : i + 1, :], 1, keepdims=True), (8, width))
            for i in range(2 * ITERS)
        ]
        field, rest, bad = coefficients(sums)
        for i, value in enumerate(field + rest):
            weights[i] = value
        loss[...] = bad

    levels, width = state.shape[1:]

    def weighted(i, x):
        return (x.reshape(levels // 8, 8, width) * weights[i]).reshape(levels, width)

    x, r = state[0], None
    for k in range(DEPTH):
        v = vectors[k, 0]
        if k < ITERS:
            x = x + weighted(k, v)
        part = weighted(ITERS + k, v)
        r = part if r is None else r + part
    new_state[0] = x
    residual[0] = r


def recombine(moments, state, vectors):
    rows, levels, width = state.shape
    block = pl.BlockSpec((1, levels, width), lambda j: (j, 0, 0))
    stack = pl.BlockSpec((DEPTH, 1, levels, width), lambda j: (0, j, 0, 0))
    whole = lambda *s: pl.BlockSpec(s, lambda j: (0,) * len(s))
    like = jax.ShapeDtypeStruct(state.shape, F32)
    return pl.pallas_call(
        recombine_kernel,
        grid=(rows,),
        out_shape=(like, like, jax.ShapeDtypeStruct((8, width), F32)),
        in_specs=[whole(16, width), block, stack],
        out_specs=(block, block, whole(8, width)),
        scratch_shapes=[pltpu.VMEM((ITERS + DEPTH, 8, width), F32)],
        compiler_params=pltpu.CompilerParams(vmem_limit_bytes=24 << 20),
        cost_estimate=pl.CostEstimate(
            flops=6 << 20, bytes_accessed=9 << 20, transcendentals=0
        ),
        name="recombine",
    )(moments, state, vectors)


def flux_kernel(first, mask, state, vapour, cosine, albedo, across, spread, weight, *rest):
    out, slanted, upright = rest[-3:]
    j = first + pl.program_id(0)
    levels = state.shape[1]
    tiles = across.shape[0] // 8

    @pl.when(mask[j] == 0)
    def _():
        out[...] = jnp.zeros_like(out)

    @pl.when(mask[j] != 0)
    def _():
        optical = vapour[0] * (1.0 + 0.5 * jnp.tanh(state[0]))
        mu = cosine[0]
        slant = LOG2E / mu
        slanted[...] = optical * -slant
        upright[...] = optical * (1.66 * LOG2E)
        total = jnp.dot(
            across[...], optical, precision=lax.Precision.HIGHEST, preferred_element_type=F32
        )
        down = jnp.log2(weight[...] * mu)
        up = down + jnp.log2(albedo[0]) - total * (slant + 1.66 * LOG2E)
        sub = lax.broadcasted_iota(jnp.int32, (8, 128), 0)
        cut = lambda x: tuple(x[8 * t : 8 * t + 8] for t in range(tiles))

        def eight_levels(i, carry):
            down, up = (list(c) for c in carry)
            result = jnp.zeros((8, 128), F32)
            for k in range(8):
                level = i * 8 + k
                o1 = jnp.broadcast_to(slanted[pl.ds(level, 1), :], (8, 128))
                o2 = jnp.broadcast_to(upright[pl.ds(level, 1), :], (8, 128))
                net = None
                for t in range(tiles):
                    a = spread[level, 8 * t : 8 * t + 8, :]
                    down[t] = down[t] + a * o1
                    up[t] = up[t] + a * o2
                    one = jnp.exp2(down[t]) - jnp.exp2(up[t])
                    net = one if net is None else net + one
                result = jnp.where(sub == k, jnp.sum(net, 0, keepdims=True), result)
            out[0, pl.ds(pl.multiple_of(i * 8, 8), 8), :] = result
            return tuple(down), tuple(up)

        lax.fori_loop(0, levels // 8, eight_levels, (cut(down), cut(up)))


def fluxes(first, count, mask, fields, tables, before):
    state = fields[0]
    rows, levels, width = state.shape
    g = tables[0].shape[0]
    block = pl.BlockSpec((1, levels, width), lambda j, m: (first + j, 0, 0))
    row = pl.BlockSpec((1, 1, width), lambda j, m: (first + j, 0, 0))
    whole = lambda *s: pl.BlockSpec(s, lambda j, m: (0,) * len(s))
    resident = pl.BlockSpec(memory_space=pltpu.VMEM)
    in_specs = [block, block, row, row, whole(g, levels), resident, whole(g, width)]
    held = () if before is None else (before,)
    if held:
        in_specs.append(pl.BlockSpec(memory_space=pl.ANY))
    return pl.pallas_call(
        functools.partial(flux_kernel, first),
        out_shape=jax.ShapeDtypeStruct(state.shape, F32),
        grid_spec=pltpu.PrefetchScalarGridSpec(
            num_scalar_prefetch=1,
            grid=(count,),
            in_specs=in_specs,
            out_specs=block,
            scratch_shapes=[pltpu.VMEM((levels, width), F32)] * 2,
        ),
        input_output_aliases={8: 0} if held else {},
        compiler_params=pltpu.CompilerParams(vmem_limit_bytes=20 << 20),
        cost_estimate=pl.CostEstimate(
            flops=count * (24 << 20), bytes_accessed=count * (6 << 20), transcendentals=count * (4 << 20)
        ),
        name="fluxes",
    )(mask, *fields, *tables, *held)


def shifted(values):
    width = values.shape[2]
    west = lax.ppermute(values[:, :, width - 1 :], GX, ring(GX, 1))
    east = lax.ppermute(values[:, :, :1], GX, ring(GX, -1))
    south = lax.ppermute(values[-1:], GY, line(GY, 1))
    north = lax.ppermute(values[:1], GY, line(GY, -1))
    wide = jnp.concatenate([west, values, east], 2)
    tall = jnp.concatenate([south, values, north], 0)
    return wide, tall


def plain(state, diff):
    wide, tall = shifted(diff)
    faces = [diff * wide[:, :, 2:], diff * wide[:, :, :-2], diff * tall[2:], diff * tall[:-2]]
    east, west, north, south = [jnp.sqrt(f) for f in faces]
    level = jnp.sqrt(diff[:, 1:] * diff[:, :-1])

    def operate(v):
        wide, tall = shifted(v)
        out = v + east * (v - wide[:, :, 2:]) + west * (v - wide[:, :, :-2])
        out = out + north * (v - tall[2:]) + south * (v - tall[:-2])
        flux = level * (v[:, 1:] - v[:, :-1])
        return out - jnp.pad(flux, ((0, 0), (0, 1), (0, 0))) + jnp.pad(flux, ((0, 0), (1, 0), (0, 0)))

    total = lambda a, b: lax.psum(lax.psum(jnp.sum(a * b), GX), GY)
    residual = state - operate(state)

    def iteration(_, carry):
        field, residual, direction, current = carry
        applied = operate(direction)
        step = current / total(direction, applied)
        field = field + step * direction
        residual = residual - step * applied
        following = total(residual, residual)
        return field, residual, residual + following / current * direction, following

    start = (state, residual, residual, total(residual, residual))
    return lax.fori_loop(0, ITERS, iteration, start)[:2]


def doubled(part, axis):
    n = lax.axis_size(axis)
    step = 1
    while step < n:
        other = lax.ppermute(part, axis, [(i, i ^ step) for i in range(n)])
        part = part + other
        step *= 2
    return part


def body(state, diff, vapour, cosine, albedo, absorption, weight, mask):
    rows, levels, width = state.shape
    g = absorption.shape[1]
    tables = (
        absorption.T,
        jnp.broadcast_to(absorption[:, :, None], (levels, g, width)),
        jnp.broadcast_to(weight[:, None], (g, width)),
    )
    fields = (state, vapour, cosine[:, None, :], albedo[:, None, :])

    to_north, to_south, to_east, to_west = edges(state, diff)
    east = lax.ppermute(to_west, GX, ring(GX, -1))
    west = lax.ppermute(to_east, GX, ring(GX, 1))
    south = lax.ppermute(to_north, GY, line(GY, 1))
    north = lax.ppermute(to_south, GY, line(GY, -1))
    sides = jnp.concatenate([east, west], 0)
    south_side = lax.ppermute(sides, GY, line(GY, 1))
    north_side = lax.ppermute(sides, GY, line(GY, -1))
    vectors, moments = basis(state, diff, north, south, east, west, north_side, south_side)
    moments = doubled(doubled(moments, GX), GY)
    new_state, residual, loss = recombine(moments, state, vectors)

    net = None
    first = 0
    for count in (6, 3) + (1,) * 7:
        net = fluxes(first, count, mask, fields, tables, net)
        first += count

    def untrusted(carry):
        return jnp.logical_not(carry[2] <= 1.0)

    def redo(carry):
        return (*plain(state, diff), jnp.ones((), F32))

    new_state, residual, _ = lax.while_loop(
        untrusted, redo, (new_state, residual, loss[0, 0])
    )
    return new_state, residual, net


def solution(mesh):
    block = P(GY, None, GX)
    in_specs = (block, block, block, P(GY, GX), P(GY, GX), P(), P(), P((GX, GY)))
    return jax.shard_map(
        body, mesh=mesh, in_specs=in_specs, out_specs=(block,) * 3, check_vma=False
    )
```

```python
import functools
import math

import jax
import jax.numpy as jnp
from jax import lax
from jax.experimental import pallas as pl
from jax.experimental.pallas import tpu as pltpu
from jax.sharding import PartitionSpec as P

ITERS = 5
DEPTH = ITERS + 1
SLOT = 16
GROUP = 8
CHUNK = 32
CENTRE = 14.0
HALF = 13.0
TRUST = 500.0
LOG2E = math.log2(math.e)
GX, GY = ("gx", "gy")
F32 = jnp.float32


def ring(axis, step):
    n = lax.axis_size(axis)
    return [(i, (i + step) % n) for i in range(n)]


def line(axis, step):
    n = lax.axis_size(axis)
    return [(i, i + step) for i in range(n) if 0 <= i + step < n]


def lanes(shape):
    return lax.broadcasted_iota(jnp.int32, shape, len(shape) - 1)


def edges_kernel(state, diff, north, south, east, west):
    rows, levels, width = state.shape
    for f, source in enumerate((state, diff)):

        @pl.loop(0, levels // CHUNK)
        def _(c):
            at = pl.ds(pl.multiple_of(c * CHUNK, CHUNK), CHUNK)
            lane = lanes((CHUNK, width))
            for h, first in enumerate(block_rows(rows)):
                to_west = jnp.zeros((CHUNK, width), F32)
                to_east = jnp.zeros((CHUNK, width), F32)
                for i in range(GROUP):
                    r = first + i
                    if -DEPTH <= r < 0:
                        x = south[f * DEPTH + DEPTH + r, at, :]
                    elif 0 <= r < rows:
                        x = source[r, at, :]
                    elif rows <= r < rows + DEPTH:
                        x = north[f * DEPTH + r - rows, at, :]
                    else:
                        continue
                    place = i * SLOT + DEPTH
                    mine = (lane >= place) & (lane < place + DEPTH)
                    to_west = jnp.where(mine, pltpu.roll(x, place, 1), to_west)
                    place = i * SLOT + 8 - DEPTH
                    mine = (lane >= place) & (lane < place + DEPTH)
                    moved = pltpu.roll(x, (place + DEPTH) % width, 1)
                    to_east = jnp.where(mine, moved, to_east)
                west[h, f, at, :] = to_west
                east[h, f, at, :] = to_east


def block_rows(rows):
    return 0, GROUP, rows, -GROUP


def edges(state, diff, north, south):
    rows, levels, width = state.shape
    thin = jax.ShapeDtypeStruct((4, 2, levels, width), F32)
    return pl.pallas_call(
        edges_kernel,
        out_shape=(thin, thin),
        compiler_params=pltpu.CompilerParams(vmem_limit_bytes=10 << 20),
        cost_estimate=pl.CostEstimate(
            flops=1 << 20, bytes_accessed=4 << 20, transcendentals=0
        ),
        name="edges",
    )(state, diff, north, south)


def basis_kernel(
    state, diff, north, south, east, west, vectors, moments, *work
):
    ce, cw, cn, cl, va, vb, flow, se, sn, sl, sa, sb, sc, joint = work
    rows, levels, width = state.shape
    total = rows + 2 * DEPTH
    tiles = levels // 8
    lane = lanes((8, width))
    in_slot = lane % SLOT

    def sparse(t):
        return pl.ds(t, 8, stride=tiles)

    def root(x):
        return jnp.sqrt(x * (2.0 / HALF))

    def up_level(x):
        return pltpu.roll(x, 7, 0)

    def down_level(x):
        return pltpu.roll(x, 1, 0)

    for f, (own, target) in enumerate(((state, va), (diff, vb))):
        fix = root if f else (lambda x: x)
        for base, source, count in (
            (0, south, DEPTH),
            (DEPTH, own, rows),
            (DEPTH + rows, north, DEPTH),
        ):
            skip = f * DEPTH if count == DEPTH else 0

            @pl.loop(0, count)
            def _(r):
                for t in range(tiles):
                    target[base + r, t] = fix(source[skip + r, sparse(t), :])

    for f, (main, side) in enumerate(((va, sa), (vb, sb))):
        fix = root if f else (lambda x: x)
        for ring_block, base in enumerate(block_rows(rows)):
            first = base + DEPTH

            def strip(t):
                at = sparse(t)
                e, w = east[ring_block, f, at, :], west[ring_block, f, at, :]
                e, w = fix(e), fix(w)
                slots = [i for i in range(GROUP) if 0 <= first + i < total]
                x = [main[first + i, t] for i in slots]
                xe = [pltpu.roll(p, i * SLOT + DEPTH, 1) for i, p in zip(slots, x)]
                xw = [pltpu.roll(p, i * SLOT + 8, 1) for i, p in zip(slots, x)]
                for i, p, q in zip(slots, xe, xw):
                    place = i * SLOT
                    e = jnp.where((lane >= place) & (lane < place + DEPTH), p, e)
                    place = i * SLOT + 8
                    w = jnp.where((lane >= place) & (lane < place + DEPTH), q, w)
                return e, w

            @pl.loop(0, tiles // 4)
            def _(turn):
                made = [strip(turn * 4 + n) for n in range(4)]
                for n, (e, w) in enumerate(made):
                    side[0, ring_block, turn * 4 + n] = e
                    side[1, ring_block, turn * 4 + n] = w

    def join(side):
        seventh = in_slot == 7
        for b in range(4):
            for t in range(tiles):
                joint[b, t] = jnp.where(seventh, side[1, b, t], side[0, b, t])

    def beyond(r):
        place = r - DEPTH + 4 * GROUP
        block, shift = (place // GROUP) % 4, (width - 7 - SLOT * (place % GROUP)) % width
        return lambda t: pltpu.roll(joint[block, t], shift, 1)

    at_end, at_start = lane == width - 1, lane == 0

    def eastward(v, j):
        return jnp.where(lane == width - 1, j, pltpu.roll(v, width - 1, 1))

    def westward(v, j):
        return jnp.where(lane == 0, j, pltpu.roll(v, 1, 1))

    def north_of(values):
        moved = [pltpu.roll(v, width - SLOT, 1) for v in values]
        cut = lane >= width - SLOT
        return [jnp.where(cut, moved[(b + 1) % 4], moved[b]) for b in range(4)]

    def south_of(values):
        moved = [pltpu.roll(v, SLOT, 1) for v in values]
        cut = lane < SLOT
        return [jnp.where(cut, moved[(b + 3) % 4], moved[b]) for b in range(4)]

    top = lax.broadcasted_iota(jnp.int32, (8, width), 0) == 7
    join(sb)

    @pl.loop(0, total)
    def _(r):
        outside = beyond(r)
        up_row = jnp.minimum(r + 1, total - 1)
        for t in range(tiles):
            q, j = vb[r, t], outside(t)
            ce[r, t] = q * eastward(q, j)
            cw[r, t] = q * westward(q, j)
            cn[r, t] = q * vb[up_row, t]
            if t + 1 < tiles:
                cl[r, t] = q * vb[r, t + 1]
            else:
                cl[r, t] = jnp.where(top, 0.0, q * up_level(vb[r, 0]))

    for s in range(2):

        for t in range(tiles):
            q = [sb[s, b, t] for b in range(4)]
            for b, n in enumerate(north_of(q)):
                se[s, b, t] = q[b] * pltpu.roll(q[b], width - 1, 1)
                sn[s, b, t] = q[b] * n

        @pl.loop(0, 4)
        def _(b):
            for t in range(tiles):
                q = sb[s, b, t]
                if t + 1 < tiles:
                    sl[s, b, t] = q * sb[s, b, t + 1]
                else:
                    sl[s, b, t] = jnp.where(top, 0.0, q * up_level(sb[s, b, 0]))

    def advanced(k, spread, v, older):
        if k == 0:
            return spread * (-0.5 * HALF)
        if k == 1:
            return 0.5 * spread + ((1.0 - CENTRE) / HALF) * v
        return spread + (2.0 * (1.0 - CENTRE) / HALF) * v - older

    def apply(k, source, older, target):
        last = k == ITERS

        def row(r, sums, own):
            outside = beyond(r)
            sums = list(sums)
            part = tiles // 2
            made = []
            for h in range(0, tiles, part):
                span = range(h, h + part)
                v = [source[r, t] for t in span]
                j = [outside(t) for t in span]
                e = [pltpu.roll(x, width - 1, 1) for x in v]
                w = [pltpu.roll(x, 1, 1) for x in v]
                under = source[r, h - 1] if h else source[r, tiles - 1]
                over = source[r, h + part] if h + part < tiles else up_level(source[r, 0])
                if h:
                    rise = cl[r, h - 1] * (under - v[0])
                else:
                    rise = down_level(cl[r, tiles - 1] * (under - up_level(v[0])))
                above = v[1:] + [over]
                for n, t in enumerate(span):
                    x = v[n]
                    spread = ce[r, t] * (x - jnp.where(at_end, j[n], e[n]))
                    spread += cw[r, t] * (x - jnp.where(at_start, j[n], w[n]))
                    crossing = cn[r, t] * (x - source[r + 1, t])
                    climb = cl[r, t] * (x - above[n])
                    spread += (crossing - flow[t]) + (climb - rise)
                    rise = climb
                    new = advanced(k, spread, x, older[r, t] if k > 1 else None)
                    made.append((t, crossing, new))
                    if own:
                        products = ([] if last else [new * new]) + ([new * x] if k else [])
                        sums = [p + q for p, q in zip(sums, products)]
                for t, crossing, new in made:
                    flow[t] = crossing
                    target[r, t] = new
                made = []
            return tuple(sums)

        for t in range(tiles):
            flow[t] = cn[k, t] * (source[k, t] - source[k + 1, t])

        def halo(r):
            row(r, (), False)

        if not last:
            pl.loop(k + 1, DEPTH)(halo)
        zero = jnp.zeros((8, width), F32)
        start = (zero,) * (1 if k in (0, ITERS) else 2)
        sums = lax.fori_loop(DEPTH, DEPTH + rows, lambda r, c: row(r, c, True), start)
        if not last:
            pl.loop(DEPTH + rows, total - 1 - k)(halo)
        places = ([] if last else [2 * k]) + ([2 * k - 1] if k else [])
        for place, part in zip(places, sums):
            moments[place : place + 1, :] = jnp.sum(part, 0, keepdims=True)

    def apply_sides(k, source, older, target):
        def block(s, t):
            v = [source[s, b, t] for b in range(4)]
            north = north_of(v)
            crossing = [sn[s, b, t] * (x - n) for b, (x, n) in enumerate(zip(v, north))]
            out = [
                se[s, b, t] * (v[b] - pltpu.roll(v[b], width - 1, 1)) for b in range(4)
            ]
            arrived = south_of(crossing)
            made = []
            for b in range(4):
                spread = out[b] - pltpu.roll(out[b], 1, 1) + (crossing[b] - arrived[b])
                if t + 1 < tiles:
                    over = source[s, b, t + 1]
                else:
                    over = up_level(source[s, b, 0])
                if t:
                    rise = sl[s, b, t - 1] * (source[s, b, t - 1] - v[b])
                else:
                    end = tiles - 1
                    rise = down_level(sl[s, b, end] * (source[s, b, end] - up_level(v[b])))
                spread += sl[s, b, t] * (v[b] - over) - rise
                made.append(advanced(k, spread, v[b], older[s, b, t] if k > 1 else None))
            return made

        @pl.loop(0, 2)
        def _(s):
            for h in range(0, tiles, 4):
                made = [block(s, t) for t in range(h, h + 4)]
                for n, blocks in enumerate(made):
                    for b, new in enumerate(blocks):
                        target[s, b, h + n] = new

    moments[...] = jnp.zeros_like(moments)
    fields = [va] + [vectors.at[k] for k in range(DEPTH)]
    sides = (sb, sc, sa)
    for k in range(DEPTH):
        join(sides[(k - 1) % 3])
        apply(k, fields[k], fields[k - 1], fields[k + 1])
        if k < ITERS:
            apply_sides(k, sides[(k - 1) % 3], sides[(k - 2) % 3], sides[k % 3])


def basis(*arrays):
    rows, levels, width = arrays[0].shape
    total = rows + 2 * DEPTH
    tiles = levels // 8
    main = pltpu.VMEM((total, tiles, 8, width), F32)
    side = pltpu.VMEM((2, 4, tiles, 8, width), F32)
    return pl.pallas_call(
        basis_kernel,
        out_shape=(
            jax.ShapeDtypeStruct((DEPTH, total, tiles, 8, width), F32),
            jax.ShapeDtypeStruct((16, width), F32),
        ),
        scratch_shapes=[main] * 6
        + [pltpu.VMEM((tiles, 8, width), F32)]
        + [side] * 6
        + [pltpu.VMEM((4, tiles, 8, width), F32)],
        out_specs=(
            pl.BlockSpec(memory_space=pltpu.VMEM),
            pl.BlockSpec(memory_space=pltpu.VMEM),
        ),
        compiler_params=pltpu.CompilerParams(vmem_limit_bytes=34 << 20),
        cost_estimate=pl.CostEstimate(
            flops=100 << 20, bytes_accessed=14 << 20, transcendentals=0
        ),
        name="basis",
    )(*arrays)


def coefficients(sums):
    zero = jnp.zeros_like(sums[0])
    one = zero + 1.0
    mom = []
    for k in range(ITERS):
        mom.append(2.0 * sums[2 * k] - (mom[0] if k else sums[0]))
        mom.append(2.0 * sums[2 * k + 1] - (mom[1] if k else sums[1]))

    gram = {}
    for j in range(DEPTH):
        for k in range(j, DEPTH):
            if j + k < 2 * ITERS:
                gram[j, k] = gram[k, j] = 0.5 * (mom[j + k] + mom[k - j])

    def inner(a, b):
        value = size = zero
        for j, p in enumerate(a):
            for k, q in enumerate(b):
                term = p * q * gram[j, k]
                value, size = value + term, size + jnp.abs(term)
        return value, size

    def image(p):
        out = [CENTRE * q for q in p] + [zero]
        for k, q in enumerate(p):
            if k == 0:
                out[1] = out[1] + HALF * q
            else:
                out[k - 1] = out[k - 1] + 0.5 * HALF * q
                out[k + 1] = out[k + 1] + 0.5 * HALF * q
        return out

    def combined(a, scale, b):
        n = max(len(a), len(b))
        a, b = [list(x) + [zero] * (n - len(x)) for x in (a, b)]
        return [p + scale * q for p, q in zip(a, b)]

    residual, direction, field = [one], [one], []
    current, loss = mom[0], one
    for k in range(ITERS):
        applied = image(direction)
        curvature, size = inner(direction, applied)
        loss = jnp.maximum(loss, jnp.where(size < TRUST * curvature, one, 2.0 * one))
        step = current / curvature
        field = combined(field, step, direction)
        residual = combined(residual, -step, applied)
        if k < ITERS - 1:
            following, size = inner(residual, residual)
            loss = jnp.maximum(loss, jnp.where(size < TRUST * following, one, 2.0 * one))
            direction = combined(residual, following / current, direction)
            current = following
    return field, residual, loss


def recombine_kernel(moments, state, vectors, new_state, residual, loss, weights):
    @pl.when(pl.program_id(0) == 0)
    def _():
        width = moments.shape[1]
        sums = [
            jnp.broadcast_to(jnp.sum(moments[i : i + 1, :], 1, keepdims=True), (8, width))
            for i in range(2 * ITERS)
        ]
        field, rest, bad = coefficients(sums)
        for i, value in enumerate(field + rest):
            weights[i] = value
        loss[...] = bad

    count = new_state.shape[0]
    tiles = state.shape[1] // 8
    for n in range(count):
        j = pl.program_id(0) * count + n
        for i in range(tiles):
            at = slice(8 * i, 8 * i + 8)
            ordered = pl.ds((8 * i) % tiles * 8 + 8 * i // tiles, 8, stride=8)
            x, r = state[j, at, :], None
            for k in range(DEPTH):
                v = vectors[k, DEPTH + j, ordered, :]
                if k < ITERS:
                    x = x + weights[k] * v
                part = weights[ITERS + k] * v
                r = part if r is None else r + part
            new_state[n, at, :] = x
            residual[n, at, :] = r


def recombine(moments, state, vectors):
    rows, levels, width = state.shape
    block = pl.BlockSpec((4, levels, width), lambda j: (j, 0, 0))
    resident = pl.BlockSpec(memory_space=pltpu.VMEM)
    vectors = vectors.reshape(*vectors.shape[:2], levels, width)
    whole = lambda *s: pl.BlockSpec(s, lambda j: (0,) * len(s))
    like = jax.ShapeDtypeStruct(state.shape, F32)
    return pl.pallas_call(
        recombine_kernel,
        grid=(rows // 4,),
        out_shape=(like, like, jax.ShapeDtypeStruct((8, width), F32)),
        in_specs=[resident] * 3,
        out_specs=(block, block, whole(8, width)),
        scratch_shapes=[pltpu.VMEM((ITERS + DEPTH, 8, width), F32)],
        compiler_params=pltpu.CompilerParams(vmem_limit_bytes=16 << 20),
        cost_estimate=pl.CostEstimate(
            flops=6 << 20, bytes_accessed=9 << 20, transcendentals=0
        ),
        name="recombine",
    )(moments, state, vectors)


def widened_kernel(eights, spread):
    count, g, _ = eights.shape

    @pl.loop(0, count)
    def _(i):
        columns = eights[i]
        for k in range(8):
            spread[i * 8 + k] = jnp.broadcast_to(columns[:, k : k + 1], spread.shape[1:])


def widened(eights, width):
    count, g, _ = eights.shape
    return pl.pallas_call(
        widened_kernel,
        out_shape=pltpu.VMEM((count * 8, g, width), F32),
        compiler_params=pltpu.CompilerParams(vmem_limit_bytes=11 << 20),
        cost_estimate=pl.CostEstimate(
            flops=2 << 20, bytes_accessed=8 << 20, transcendentals=0
        ),
        name="widened",
    )(eights)


def flux_kernel(first, mask, state, vapour, cosine, albedo, across, spread, weight, *rest):
    out, slanted, upright = rest[-3:]
    levels = state.shape[1]
    tiles = across.shape[0] // 8

    def sunlit(j):
        optical = vapour[j] * (1.0 + 0.5 * jnp.tanh(state[j]))
        mu = cosine[pl.ds(j, 1), :]
        slant = LOG2E / mu
        slanted[...] = optical * -slant
        upright[...] = optical * (1.66 * LOG2E)
        total = jnp.dot(
            across[...], optical, precision=lax.Precision.HIGHEST, preferred_element_type=F32
        )
        down = jnp.log2(weight[...] * mu)
        up = down + jnp.log2(albedo[pl.ds(j, 1), :]) - total * (slant + 1.66 * LOG2E)
        sub = lax.broadcasted_iota(jnp.int32, (8, 128), 0)
        cut = lambda x: tuple(x[8 * t : 8 * t + 8] for t in range(tiles))

        def eight_levels(i, carry):
            down, up = (list(c) for c in carry)
            result = jnp.zeros((8, 128), F32)
            for k in range(8):
                level = i * 8 + k
                o1 = jnp.broadcast_to(slanted[pl.ds(level, 1), :], (8, 128))
                o2 = jnp.broadcast_to(upright[pl.ds(level, 1), :], (8, 128))
                net = None
                for t in range(tiles):
                    a = spread[level, 8 * t : 8 * t + 8, :]
                    down[t] = down[t] + a * o1
                    up[t] = up[t] + a * o2
                    one = jnp.exp2(down[t]) - jnp.exp2(up[t])
                    net = one if net is None else net + one
                result = jnp.where(sub == k, jnp.sum(net, 0, keepdims=True), result)
            out[0, pl.ds(pl.multiple_of(i * 8, 8), 8), :] = result
            return tuple(down), tuple(up)

        lax.fori_loop(0, levels // 8, eight_levels, (cut(down), cut(up)))

    j = first + pl.program_id(0)

    @pl.when(mask[j] == 0)
    def _():
        out[...] = jnp.zeros(out.shape, F32)

    @pl.when(mask[j] != 0)
    def _():
        sunlit(j)


def fluxes(first, count, mask, fields, tables, before):
    state = fields[0]
    rows, levels, width = state.shape
    resident = pl.BlockSpec(memory_space=pltpu.VMEM)
    held = () if before is None else (before,)
    return pl.pallas_call(
        functools.partial(flux_kernel, first),
        out_shape=jax.ShapeDtypeStruct(state.shape, F32),
        grid=(count,),
        in_specs=[pl.BlockSpec(memory_space=pltpu.SMEM)]
        + [resident] * 7
        + [pl.BlockSpec(memory_space=pl.ANY)] * len(held),
        out_specs=pl.BlockSpec((1, levels, width), lambda j: (first + j, 0, 0)),
        scratch_shapes=[pltpu.VMEM((levels, width), F32)] * 2,
        input_output_aliases={8: 0} if held else {},
        compiler_params=pltpu.CompilerParams(vmem_limit_bytes=5 << 20),
        cost_estimate=pl.CostEstimate(
            flops=count * (24 << 20), bytes_accessed=count * (6 << 20), transcendentals=count * (4 << 20)
        ),
        name="fluxes",
    )(mask, *fields, *tables, *held)


def shifted(values):
    width = values.shape[2]
    west = lax.ppermute(values[:, :, width - 1 :], GX, ring(GX, 1))
    east = lax.ppermute(values[:, :, :1], GX, ring(GX, -1))
    south = lax.ppermute(values[-1:], GY, line(GY, 1))
    north = lax.ppermute(values[:1], GY, line(GY, -1))
    wide = jnp.concatenate([west, values, east], 2)
    tall = jnp.concatenate([south, values, north], 0)
    return wide, tall


def plain(state, diff):
    wide, tall = shifted(diff)
    faces = [diff * wide[:, :, 2:], diff * wide[:, :, :-2], diff * tall[2:], diff * tall[:-2]]
    east, west, north, south = [jnp.sqrt(f) for f in faces]
    level = jnp.sqrt(diff[:, 1:] * diff[:, :-1])

    def operate(v):
        wide, tall = shifted(v)
        out = v + east * (v - wide[:, :, 2:]) + west * (v - wide[:, :, :-2])
        out = out + north * (v - tall[2:]) + south * (v - tall[:-2])
        flux = level * (v[:, 1:] - v[:, :-1])
        return out - jnp.pad(flux, ((0, 0), (0, 1), (0, 0))) + jnp.pad(flux, ((0, 0), (1, 0), (0, 0)))

    total = lambda a, b: lax.psum(lax.psum(jnp.sum(a * b), GX), GY)
    residual = state - operate(state)

    def iteration(_, carry):
        field, residual, direction, current = carry
        applied = operate(direction)
        step = current / total(direction, applied)
        field = field + step * direction
        residual = residual - step * applied
        following = total(residual, residual)
        return field, residual, residual + following / current * direction, following

    start = (state, residual, residual, total(residual, residual))
    return lax.fori_loop(0, ITERS, iteration, start)[:2]


def copy_kernel(x, y):
    y[...] = x[...]


def row_major(x):
    return pl.pallas_call(
        copy_kernel, out_shape=jax.ShapeDtypeStruct(x.shape, x.dtype), name="row_major"
    )(x)


def exchanged(part, axis, distances):
    n = lax.axis_size(axis)
    return [part] + [
        lax.ppermute(part, axis, [(i, i ^ d) for i in range(n)]) for d in distances
    ]


def added(parts):
    while len(parts) > 1:
        parts = [a + b for a, b in zip(parts[::2], parts[1::2])]
    return parts[0]


def body(state, diff, vapour, cosine, albedo, absorption, weight, mask):
    rows, levels, width = state.shape
    g = absorption.shape[1]
    eights = jnp.transpose(absorption.reshape(levels // 8, 8, g), (0, 2, 1))
    tables = (
        absorption.T,
        widened(eights, width),
        jnp.broadcast_to(weight[:, None], (g, width)),
    )
    fields = (state, vapour, cosine, albedo)
    after = lax.optimization_barrier

    def both(rows):
        return jnp.concatenate([state[rows], diff[rows]], 0)

    south = lax.ppermute(both(slice(rows - DEPTH, rows)), GY, line(GY, 1))
    north = lax.ppermute(both(slice(0, DEPTH)), GY, line(GY, -1))
    net = fluxes(0, 5, mask, fields, tables, None)
    south, north, net = after((south, north, net))
    to_east, to_west = edges(state, diff, north, south)
    east = lax.ppermute(to_west, GX, ring(GX, -1))
    west = lax.ppermute(to_east, GX, ring(GX, 1))
    net = fluxes(5, 3, mask, fields, tables, net)
    east, west, net = after((east, west, net))
    vectors, moments = basis(state, diff, north, south, east, west)
    first = 8
    stages = ((GX, (1,), 1), (GX, (2, 4, 6), 2), (GY, (1, 2, 3), 2), (GY, (4, 8, 12), 3))
    for axis, distances, count in stages:
        moments, net = after((moments, net))
        parts = exchanged(moments, axis, distances)
        net = fluxes(first, count, mask, fields, tables, net)
        first += count
        parts, net = after((parts, net))
        moments = added(parts)
    new_state, residual, loss = recombine(moments, state, vectors)

    def untrusted(carry):
        return jnp.logical_not(carry[2] <= 1.0)

    def redo(carry):
        again = plain(row_major(state), row_major(diff))
        return (*map(row_major, again), jnp.ones((), F32))

    new_state, residual, _ = lax.while_loop(
        untrusted, redo, (new_state, residual, loss[0, 0])
    )
    return new_state, residual, net


def solution(mesh):
    block = P(GY, None, GX)
    in_specs = (block, block, block, P(GY, GX), P(GY, GX), P(), P(), P((GX, GY)))
    return jax.shard_map(
        body, mesh=mesh, in_specs=in_specs, out_specs=(block,) * 3, check_vma=False
    )
```

```python
import functools
import math

import jax
import jax.numpy as jnp
from jax import lax
from jax.experimental import pallas as pl
from jax.experimental.pallas import tpu as pltpu
from jax.sharding import PartitionSpec as P

ITERS = 5
DEPTH = ITERS + 1
SLOT = 16
GROUP = 8
CHUNK = 32
SPAN = 4
ROWS = 8
CENTRE = 14.0
HALF = 13.0
TRUST = 500.0
LOG2E = math.log2(math.e)
GX, GY = ("gx", "gy")
F32 = jnp.float32


def ring(axis, step):
    n = lax.axis_size(axis)
    return [(i, (i + step) % n) for i in range(n)]


def line(axis, step):
    n = lax.axis_size(axis)
    return [(i, i + step) for i in range(n) if 0 <= i + step < n]


def lanes(shape):
    return lax.broadcasted_iota(jnp.int32, shape, len(shape) - 1)


def rows_kernel(state, diff, north, south, done):
    rows = state.shape[0]
    copies = []
    for f, source in enumerate((state, diff)):
        to = pl.ds(f * DEPTH, DEPTH)
        copies.append((source.at[pl.ds(rows - DEPTH, DEPTH)], north.at[to]))
        copies.append((source.at[pl.ds(0, DEPTH)], south.at[to]))
    copies = [pltpu.make_async_copy(x, y, done.at[i]) for i, (x, y) in enumerate(copies)]
    for copy in copies:
        copy.start()
    for copy in copies:
        copy.wait()


def outer_rows(state, diff):
    rows, levels, width = state.shape
    tall = jax.ShapeDtypeStruct((2 * DEPTH, levels, width), F32)
    anywhere = pl.BlockSpec(memory_space=pl.ANY)
    return pl.pallas_call(
        rows_kernel,
        out_shape=(tall, tall),
        in_specs=[anywhere] * 2,
        out_specs=(pl.BlockSpec(memory_space=pltpu.VMEM),) * 2,
        scratch_shapes=[pltpu.SemaphoreType.DMA((4,))],
        compiler_params=pltpu.CompilerParams(vmem_limit_bytes=3 << 20),
        name="outer_rows",
    )(state, diff)


def edges_kernel(state, diff, north, south, packed):
    rows, levels, width = state.shape
    for f, source in enumerate((state, diff)):

        @pl.loop(0, levels // CHUNK)
        def _(c):
            at = pl.ds(pl.multiple_of(c * CHUNK, CHUNK), CHUNK)
            lane = lanes((CHUNK, width))
            for h, first in enumerate(block_rows(rows)):
                both = jnp.zeros((CHUNK, width), F32)
                for i in range(GROUP):
                    r = first + i
                    if -DEPTH <= r < 0:
                        x = south[f * DEPTH + DEPTH + r, at, :]
                    elif 0 <= r < rows:
                        x = source[r, at, :]
                    elif rows <= r < rows + DEPTH:
                        x = north[f * DEPTH + r - rows, at, :]
                    else:
                        continue
                    place = i * SLOT
                    mine = (lane >= place) & (lane < place + 2 * DEPTH)
                    both = jnp.where(mine, pltpu.roll(x, place + DEPTH, 1), both)
                packed[h, f, at, :] = both


def block_rows(rows):
    return 0, GROUP, rows, -GROUP


def edges(state, diff, north, south):
    rows, levels, width = state.shape
    thin = jax.ShapeDtypeStruct((4, 2, levels, width), F32)
    return pl.pallas_call(
        edges_kernel,
        out_shape=thin,
        compiler_params=pltpu.CompilerParams(vmem_limit_bytes=10 << 20),
        cost_estimate=pl.CostEstimate(
            flops=1 << 20, bytes_accessed=4 << 20, transcendentals=0
        ),
        name="edges",
    )(state, diff, north, south)


def basis_kernel(
    state, diff, north, south, packed, east, west, vectors, moments, *work
):
    ce, cw, cn, cl, va, vb, flow, se, sw, sn, ss, sl, sa, sb, sc, joint = work
    rows, levels, width = state.shape
    total = rows + 2 * DEPTH
    tiles = levels // 8
    lane = lanes((8, width))
    in_slot = lane % SLOT

    def sparse(t):
        return pl.ds(t, 8, stride=tiles)

    def root(x):
        return jnp.sqrt(x * (2.0 / HALF))

    def up_level(x):
        return pltpu.roll(x, 7, 0)

    def down_level(x):
        return pltpu.roll(x, 1, 0)

    for f, (own, target) in enumerate(((state, va), (diff, vb))):
        fix = root if f else (lambda x: x)
        for base, source, count in (
            (0, south, DEPTH),
            (DEPTH, own, rows),
            (DEPTH + rows, north, DEPTH),
        ):
            skip = f * DEPTH if count == DEPTH else 0

            @pl.loop(0, count)
            def _(r):
                for t in range(tiles):
                    target[base + r, t] = fix(source[skip + r, sparse(t), :])

    near = in_slot < DEPTH
    for f, side in enumerate((sa, sb)):
        fix = root if f else (lambda x: x)
        for b in range(4):
            for t in range(tiles):
                own = packed[b, f, sparse(t), :]
                side[0, b, t] = fix(jnp.where(near, own, east[b, f, sparse(t), :]))
                side[1, b, t] = fix(jnp.where(near, west[b, f, sparse(t), :], own))

    def join(side):
        seventh = in_slot == 7
        for b in range(4):
            for t in range(tiles):
                joint[b, t] = jnp.where(seventh, pltpu.roll(side[1, b, t], 2, 1), side[0, b, t])

    def beyond(r):
        place = r - DEPTH + 4 * GROUP
        block, shift = (place // GROUP) % 4, (width - 7 - SLOT * (place % GROUP)) % width
        return lambda t: pltpu.roll(joint[block, t], shift, 1)

    at_end, at_start = lane == width - 1, lane == 0

    def eastward(v, j):
        return jnp.where(lane == width - 1, j, pltpu.roll(v, width - 1, 1))

    def westward(v, j):
        return jnp.where(lane == 0, j, pltpu.roll(v, 1, 1))

    def north_of(values):
        moved = [pltpu.roll(v, width - SLOT, 1) for v in values]
        cut = lane >= width - SLOT
        return [jnp.where(cut, moved[(b + 1) % 4], moved[b]) for b in range(4)]

    def south_of(values):
        moved = [pltpu.roll(v, SLOT, 1) for v in values]
        cut = lane < SLOT
        return [jnp.where(cut, moved[(b + 3) % 4], moved[b]) for b in range(4)]

    top = lax.broadcasted_iota(jnp.int32, (8, width), 0) == 7
    join(sb)

    @pl.loop(0, total // 4)
    def _(turn):
        for r in [turn * 4 + n for n in range(4)]:
            outside = beyond(r)
            up_row = jnp.minimum(r + 1, total - 1)
            q = [vb[r, t] for t in range(tiles)]
            j = [outside(t) for t in range(tiles)]
            above = q[1:] + [jnp.where(top, 0.0, up_level(q[0]))]
            for t in range(tiles):
                ce[r, t] = q[t] * eastward(q[t], j[t])
                cw[r, t] = q[t] * westward(q[t], j[t])
                cn[r, t] = q[t] * vb[up_row, t]
                cl[r, t] = q[t] * above[t]

    for s in range(2):

        for t in range(tiles):
            q = [sb[s, b, t] for b in range(4)]
            for b, (n, d) in enumerate(zip(north_of(q), south_of(q))):
                se[s, b, t] = q[b] * pltpu.roll(q[b], width - 1, 1)
                sw[s, b, t] = q[b] * pltpu.roll(q[b], 1, 1)
                sn[s, b, t] = q[b] * n
                ss[s, b, t] = q[b] * d

        @pl.loop(0, 4)
        def _(b):
            for t in range(tiles):
                q = sb[s, b, t]
                if t + 1 < tiles:
                    sl[s, b, t] = q * sb[s, b, t + 1]
                else:
                    sl[s, b, t] = jnp.where(top, 0.0, q * up_level(sb[s, b, 0]))

    def advanced(k, spread, v, older):
        if k == 0:
            return spread * (-0.5 * HALF)
        if k == 1:
            return 0.5 * spread + ((1.0 - CENTRE) / HALF) * v
        return spread + (2.0 * (1.0 - CENTRE) / HALF) * v - older

    def apply(k, source, older, target):
        last = k == ITERS

        def several(first, count, sums, own):
            sums = list(sums)
            crossed = [flow[t] for t in range(tiles)]
            for r in [first + n for n in range(count)]:
                outside = beyond(r)
                v = [source[r, t] for t in range(tiles)]
                j = [outside(t) for t in range(tiles)]
                e = [pltpu.roll(x, width - 1, 1) for x in v]
                w = [pltpu.roll(x, 1, 1) for x in v]
                above = v[1:] + [up_level(v[0])]
                rise = down_level(cl[r, tiles - 1] * (v[-1] - above[-1]))
                made = []
                for t, x in enumerate(v):
                    spread = ce[r, t] * (x - jnp.where(at_end, j[t], e[t]))
                    spread += cw[r, t] * (x - jnp.where(at_start, j[t], w[t]))
                    crossing = cn[r, t] * (x - source[r + 1, t])
                    climb = cl[r, t] * (x - above[t])
                    spread += (crossing - crossed[t]) + (climb - rise)
                    crossed[t], rise = crossing, climb
                    new = advanced(k, spread, x, older[r, t] if k > 1 else None)
                    made.append(new)
                    if own:
                        products = ([] if last else [new * new]) + ([new * x] if k else [])
                        sums = [p + q for p, q in zip(sums, products)]
                for t, new in enumerate(made):
                    target[r, t] = new
            for t in range(tiles):
                flow[t] = crossed[t]
            return tuple(sums)

        for t in range(tiles):
            flow[t] = cn[k, t] * (source[k, t] - source[k + 1, t])

        if not last:
            several(k + 1, DEPTH - k - 1, (), False)
        zero = jnp.zeros((8, width), F32)
        start = (zero,) * (1 if k in (0, ITERS) else 2)
        sums = lax.fori_loop(
            0,
            rows // ROWS,
            lambda n, c: several(DEPTH + n * ROWS, ROWS, c, True),
            start,
        )
        if not last:
            several(DEPTH + rows, DEPTH - k - 1, (), False)
        places = ([] if last else [2 * k]) + ([2 * k - 1] if k else [])
        for place, part in zip(places, sums):
            moments[place : place + 1, :] = jnp.sum(part, 0, keepdims=True)

    def apply_sides(k, source, older, target):
        def blocks(s, span):
            v = {(b, t): source[s, b, t] for t in span for b in range(4)}
            e = {p: pltpu.roll(x, width - 1, 1) for p, x in v.items()}
            w = {p: pltpu.roll(x, 1, 1) for p, x in v.items()}
            n, d = {}, {}
            for t in span:
                column = [v[b, t] for b in range(4)]
                for b, (x, y) in enumerate(zip(north_of(column), south_of(column))):
                    n[b, t], d[b, t] = x, y
            made = {}
            for b in range(4):
                t = span[0]
                if t:
                    rise = sl[s, b, t - 1] * (source[s, b, t - 1] - v[b, t])
                else:
                    end = tiles - 1
                    rise = sl[s, b, end] * (source[s, b, end] - up_level(v[b, t]))
                    rise = down_level(rise)
                for t in span:
                    x = v[b, t]
                    if t + 1 < tiles:
                        over = v[b, t + 1] if t + 1 in span else source[s, b, t + 1]
                    else:
                        over = up_level(source[s, b, 0])
                    climb = sl[s, b, t] * (x - over)
                    spread = se[s, b, t] * (x - e[b, t]) + sw[s, b, t] * (x - w[b, t])
                    spread += sn[s, b, t] * (x - n[b, t]) + ss[s, b, t] * (x - d[b, t])
                    spread += climb - rise
                    rise = climb
                    last = older[s, b, t] if k > 1 else None
                    made[b, t] = advanced(k, spread, x, last)
            return made

        @pl.loop(0, 2)
        def _(s):
            for h in range(0, tiles, SPAN):
                for (b, t), new in blocks(s, range(h, h + SPAN)).items():
                    target[s, b, t] = new

    moments[...] = jnp.zeros_like(moments)
    fields = [va] + [vectors.at[k] for k in range(DEPTH)]
    sides = (sb, sc, sa)
    for k in range(DEPTH):
        join(sides[(k - 1) % 3])
        apply(k, fields[k], fields[k - 1], fields[k + 1])
        if k < ITERS:
            apply_sides(k, sides[(k - 1) % 3], sides[(k - 2) % 3], sides[k % 3])


def basis(*arrays):
    rows, levels, width = arrays[0].shape
    total = rows + 2 * DEPTH
    tiles = levels // 8
    main = pltpu.VMEM((total, tiles, 8, width), F32)
    side = pltpu.VMEM((2, 4, tiles, 8, width), F32)
    return pl.pallas_call(
        basis_kernel,
        out_shape=(
            jax.ShapeDtypeStruct((DEPTH, total, tiles, 8, width), F32),
            jax.ShapeDtypeStruct((16, width), F32),
        ),
        scratch_shapes=[main] * 6
        + [pltpu.VMEM((tiles, 8, width), F32)]
        + [side] * 8
        + [pltpu.VMEM((4, tiles, 8, width), F32)],
        out_specs=(
            pl.BlockSpec(memory_space=pltpu.VMEM),
            pl.BlockSpec(memory_space=pltpu.VMEM),
        ),
        compiler_params=pltpu.CompilerParams(vmem_limit_bytes=34 << 20),
        cost_estimate=pl.CostEstimate(
            flops=100 << 20, bytes_accessed=14 << 20, transcendentals=0
        ),
        name="basis",
    )(*arrays)


def coefficients(sums):
    zero = jnp.zeros_like(sums[0])
    one = zero + 1.0
    mom = []
    for k in range(ITERS):
        mom.append(2.0 * sums[2 * k] - (mom[0] if k else sums[0]))
        mom.append(2.0 * sums[2 * k + 1] - (mom[1] if k else sums[1]))

    gram = {}
    for j in range(DEPTH):
        for k in range(j, DEPTH):
            if j + k < 2 * ITERS:
                gram[j, k] = gram[k, j] = 0.5 * (mom[j + k] + mom[k - j])

    def inner(a, b):
        value = size = zero
        for j, p in enumerate(a):
            for k, q in enumerate(b):
                term = p * q * gram[j, k]
                value, size = value + term, size + jnp.abs(term)
        return value, size

    def image(p):
        out = [CENTRE * q for q in p] + [zero]
        for k, q in enumerate(p):
            if k == 0:
                out[1] = out[1] + HALF * q
            else:
                out[k - 1] = out[k - 1] + 0.5 * HALF * q
                out[k + 1] = out[k + 1] + 0.5 * HALF * q
        return out

    def combined(a, scale, b):
        n = max(len(a), len(b))
        a, b = [list(x) + [zero] * (n - len(x)) for x in (a, b)]
        return [p + scale * q for p, q in zip(a, b)]

    residual, direction, field = [one], [one], []
    current, loss = mom[0], one
    for k in range(ITERS):
        applied = image(direction)
        curvature, size = inner(direction, applied)
        loss = jnp.maximum(loss, jnp.where(size < TRUST * curvature, one, 2.0 * one))
        step = current / curvature
        field = combined(field, step, direction)
        residual = combined(residual, -step, applied)
        if k < ITERS - 1:
            following, size = inner(residual, residual)
            loss = jnp.maximum(loss, jnp.where(size < TRUST * following, one, 2.0 * one))
            direction = combined(residual, following / current, direction)
            current = following
    return field, residual, loss


def recombine_kernel(moments, state, vectors, new_state, residual, loss, weights):
    @pl.when(pl.program_id(0) == 0)
    def _():
        width = moments.shape[1]
        sums = [
            jnp.broadcast_to(jnp.sum(moments[i : i + 1, :], 1, keepdims=True), (8, width))
            for i in range(2 * ITERS)
        ]
        field, rest, bad = coefficients(sums)
        for i, value in enumerate(field + rest):
            weights[i] = value
        loss[...] = bad

    count = new_state.shape[0]
    tiles = state.shape[1] // 8
    for n in range(count):
        j = pl.program_id(0) * count + n
        for i in range(tiles):
            at = slice(8 * i, 8 * i + 8)
            ordered = pl.ds((8 * i) % tiles * 8 + 8 * i // tiles, 8, stride=8)
            x, r = state[j, at, :], None
            for k in range(DEPTH):
                v = vectors[k, DEPTH + j, ordered, :]
                if k < ITERS:
                    x = x + weights[k] * v
                part = weights[ITERS + k] * v
                r = part if r is None else r + part
            new_state[n, at, :] = x
            residual[n, at, :] = r


def recombine(moments, state, vectors):
    rows, levels, width = state.shape
    block = pl.BlockSpec((4, levels, width), lambda j: (j, 0, 0))
    resident = pl.BlockSpec(memory_space=pltpu.VMEM)
    vectors = vectors.reshape(*vectors.shape[:2], levels, width)
    whole = lambda *s: pl.BlockSpec(s, lambda j: (0,) * len(s))
    like = jax.ShapeDtypeStruct(state.shape, F32)
    return pl.pallas_call(
        recombine_kernel,
        grid=(rows // 4,),
        out_shape=(like, like, jax.ShapeDtypeStruct((8, width), F32)),
        in_specs=[resident] * 3,
        out_specs=(block, block, whole(8, width)),
        scratch_shapes=[pltpu.VMEM((ITERS + DEPTH, 8, width), F32)],
        compiler_params=pltpu.CompilerParams(vmem_limit_bytes=16 << 20),
        cost_estimate=pl.CostEstimate(
            flops=6 << 20, bytes_accessed=9 << 20, transcendentals=0
        ),
        name="recombine",
    )(moments, state, vectors)


def tables_kernel(absorption, weight, state, vapour, optical, across, spread, weights):
    levels, g = absorption.shape
    width = state.shape[2]
    turned = jnp.transpose(absorption[...])
    across[...] = turned
    weights[...] = jnp.transpose(jnp.broadcast_to(weight[...], (width, g)))
    for level in range(levels):
        spread[level] = jnp.broadcast_to(turned[:, level : level + 1], (g, width))

    @pl.loop(0, state.shape[0])
    def _(r):
        optical[r] = vapour[r] * (1.0 + 0.5 * jnp.tanh(state[r]))


def flux_tables(absorption, weight, state, vapour):
    rows, levels, width = state.shape
    g = absorption.shape[1]
    return pl.pallas_call(
        tables_kernel,
        out_shape=(
            pltpu.VMEM(state.shape, F32),
            pltpu.VMEM((g, levels), F32),
            pltpu.VMEM((levels, g, width), F32),
            pltpu.VMEM((g, width), F32),
        ),
        compiler_params=pltpu.CompilerParams(vmem_limit_bytes=13 << 20),
        cost_estimate=pl.CostEstimate(
            flops=2 << 20, bytes_accessed=10 << 20, transcendentals=1 << 18
        ),
        name="flux_tables",
    )(absorption, weight[None], state, vapour)


def flux_kernel(first, mask, amounts, cosine, albedo, across, spread, weight, *rest):
    out, slanted, upright = rest[-3:]
    levels = amounts.shape[1]
    tiles = across.shape[0] // 8

    def sunlit(j):
        optical = amounts[j]
        mu = cosine[pl.ds(j, 1), :]
        slant = LOG2E / mu
        slanted[...] = optical * -slant
        upright[...] = optical * (1.66 * LOG2E)
        total = jnp.dot(
            across[...], optical, precision=lax.Precision.HIGHEST, preferred_element_type=F32
        )
        down = jnp.log2(weight[...] * mu)
        up = down + jnp.log2(albedo[pl.ds(j, 1), :]) - total * (slant + 1.66 * LOG2E)
        sub = lax.broadcasted_iota(jnp.int32, (8, 128), 0)
        cut = lambda x: tuple(x[8 * t : 8 * t + 8] for t in range(tiles))

        def eight_levels(i, carry):
            down, up = (list(c) for c in carry)
            result = jnp.zeros((8, 128), F32)
            for k in range(8):
                level = i * 8 + k
                o1 = jnp.broadcast_to(slanted[pl.ds(level, 1), :], (8, 128))
                o2 = jnp.broadcast_to(upright[pl.ds(level, 1), :], (8, 128))
                net = None
                for t in range(tiles):
                    a = spread[level, 8 * t : 8 * t + 8, :]
                    down[t] = down[t] + a * o1
                    up[t] = up[t] + a * o2
                    one = jnp.exp2(down[t]) - jnp.exp2(up[t])
                    net = one if net is None else net + one
                result = jnp.where(sub == k, jnp.sum(net, 0, keepdims=True), result)
            out[0, pl.ds(pl.multiple_of(i * 8, 8), 8), :] = result
            return tuple(down), tuple(up)

        lax.fori_loop(0, levels // 8, eight_levels, (cut(down), cut(up)))

    j = first + pl.program_id(0)

    @pl.when(mask[j] == 0)
    def _():
        out[...] = jnp.zeros(out.shape, F32)

    @pl.when(mask[j] != 0)
    def _():
        sunlit(j)


def fluxes(first, count, mask, fields, tables, before):
    rows, levels, width = fields[0].shape
    resident = pl.BlockSpec(memory_space=pltpu.VMEM)
    held = () if before is None else (before,)
    return pl.pallas_call(
        functools.partial(flux_kernel, first),
        out_shape=jax.ShapeDtypeStruct(fields[0].shape, F32),
        grid=(count,),
        in_specs=[pl.BlockSpec(memory_space=pltpu.SMEM)]
        + [resident] * 6
        + [pl.BlockSpec(memory_space=pl.ANY)] * len(held),
        out_specs=pl.BlockSpec((1, levels, width), lambda j: (first + j, 0, 0)),
        scratch_shapes=[pltpu.VMEM((levels, width), F32)] * 2,
        input_output_aliases={7: 0} if held else {},
        compiler_params=pltpu.CompilerParams(vmem_limit_bytes=5 << 20),
        cost_estimate=pl.CostEstimate(
            flops=count * (24 << 20), bytes_accessed=count * (6 << 20), transcendentals=count * (4 << 20)
        ),
        name="fluxes",
    )(mask, *fields, *tables, *held)


def shifted(values):
    width = values.shape[2]
    west = lax.ppermute(values[:, :, width - 1 :], GX, ring(GX, 1))
    east = lax.ppermute(values[:, :, :1], GX, ring(GX, -1))
    south = lax.ppermute(values[-1:], GY, line(GY, 1))
    north = lax.ppermute(values[:1], GY, line(GY, -1))
    wide = jnp.concatenate([west, values, east], 2)
    tall = jnp.concatenate([south, values, north], 0)
    return wide, tall


def plain(state, diff):
    wide, tall = shifted(diff)
    faces = [diff * wide[:, :, 2:], diff * wide[:, :, :-2], diff * tall[2:], diff * tall[:-2]]
    east, west, north, south = [jnp.sqrt(f) for f in faces]
    level = jnp.sqrt(diff[:, 1:] * diff[:, :-1])

    def operate(v):
        wide, tall = shifted(v)
        out = v + east * (v - wide[:, :, 2:]) + west * (v - wide[:, :, :-2])
        out = out + north * (v - tall[2:]) + south * (v - tall[:-2])
        flux = level * (v[:, 1:] - v[:, :-1])
        return out - jnp.pad(flux, ((0, 0), (0, 1), (0, 0))) + jnp.pad(flux, ((0, 0), (1, 0), (0, 0)))

    total = lambda a, b: lax.psum(lax.psum(jnp.sum(a * b), GX), GY)
    residual = state - operate(state)

    def iteration(_, carry):
        field, residual, direction, current = carry
        applied = operate(direction)
        step = current / total(direction, applied)
        field = field + step * direction
        residual = residual - step * applied
        following = total(residual, residual)
        return field, residual, residual + following / current * direction, following

    start = (state, residual, residual, total(residual, residual))
    return lax.fori_loop(0, ITERS, iteration, start)[:2]


def copy_kernel(x, y):
    y[...] = x[...]


def row_major(x):
    return pl.pallas_call(
        copy_kernel, out_shape=jax.ShapeDtypeStruct(x.shape, x.dtype), name="row_major"
    )(x)


def exchanged(part, axis, distances):
    n = lax.axis_size(axis)
    return [part] + [
        lax.ppermute(part, axis, [(i, i ^ d) for i in range(n)]) for d in distances
    ]


def added(parts):
    while len(parts) > 1:
        parts = [a + b for a, b in zip(parts[::2], parts[1::2])]
    return parts[0]


def body(state, diff, vapour, cosine, albedo, absorption, weight, mask):
    after = lax.optimization_barrier

    to_north, to_south = outer_rows(state, diff)
    south = lax.ppermute(to_north, GY, line(GY, 1))
    north = lax.ppermute(to_south, GY, line(GY, -1))
    optical, *tables = flux_tables(absorption, weight, state, vapour)
    fields = (optical, cosine, albedo)
    net = fluxes(0, 5, mask, fields, tables, None)
    south, north, net = after((south, north, net))
    packed = edges(state, diff, north, south)
    east = lax.ppermute(packed, GX, ring(GX, -1))
    west = lax.ppermute(packed, GX, ring(GX, 1))
    net = fluxes(5, 3, mask, fields, tables, net)
    east, west, net = after((east, west, net))
    vectors, moments = basis(state, diff, north, south, packed, east, west)
    first = 8
    stages = ((GX, (1,), 1), (GX, (2, 4, 6), 2), (GY, (1, 2, 3), 2), (GY, (4, 8, 12), 3))
    for axis, distances, count in stages:
        moments, net = after((moments, net))
        parts = exchanged(moments, axis, distances)
        net = fluxes(first, count, mask, fields, tables, net)
        first += count
        parts, net = after((parts, net))
        moments = added(parts)
    new_state, residual, loss = recombine(moments, state, vectors)

    def untrusted(carry):
        return jnp.logical_not(carry[2] <= 1.0)

    def redo(carry):
        again = plain(row_major(state), row_major(diff))
        return (*map(row_major, again), jnp.ones((), F32))

    new_state, residual, _ = lax.while_loop(
        untrusted, redo, (new_state, residual, loss[0, 0])
    )
    return new_state, residual, net


def solution(mesh):
    block = P(GY, None, GX)
    in_specs = (block, block, block, P(GY, GX), P(GY, GX), P(), P(), P((GX, GY)))
    return jax.shard_map(
        body, mesh=mesh, in_specs=in_specs, out_specs=(block,) * 3, check_vma=False
    )
```
